768 devices in a mesh: pipe: 4 (over y_hi), win: 48 (over z, y_lo, core), head: 4 (over x).
Axes of the slice: x: 4, y: 8 (y_hi: 4, y_lo: 2; y = y_hi * 2 + y_lo), z: 12, core: 2. Of those that a mesh axis runs over, the one named last changes fastest.
Arguments:
- stream: bfloat16 [8, 1536, 2048], P('head', 'win'), may hold values from -16 to 16
- score_scale: float32 [4, 2048], P('pipe'), may hold values from -12 to 12
- value_weight: bfloat16 [4, 2048, 2048], P('pipe', None, 'head'), may hold values from -0.125 to 0.125
- out_weight: bfloat16 [4, 2048, 2048], P('pipe', 'head'), may hold values from -0.25 to 0.25
Outputs:
- sections: bfloat16 [4, 8, 1536, 2048], P('pipe', None, 'win', 'head')
The draws below stay inside these ranges and needn't reach their ends.
All inputs are finite; a program needn't handle non-finite values.
Results may differ from the reference program's by a relative error of at most 0.03.
Values may be sent and summed in bfloat16 or wider, within the bound.
A program may use at most 32 MiB of HBM per device.

```python
import math
import jax
import jax.numpy as jnp
from jax import lax

HEADS = 16
HEAD_DIM = 128
WIN = 32
ROWS = 8
D = 2048
COLS = 1536
SECTIONS = 4
N_HEAD = 4


def scale_pattern(key):
    return 2.0 * jax.random.normal(jax.random.fold_in(key, 11), (SECTIONS, HEADS * HEAD_DIM), jnp.float32)


def draw_score_scale(key, part):
    return jnp.clip(scale_pattern(key), -12.0, 12.0)


def draw_stream(key, part):
    channels = HEADS * HEAD_DIM
    return jnp.clip(jax.random.normal(jax.random.fold_in(key, 14), (ROWS, COLS, channels), jnp.float32), -6.0, 6.0).astype(jnp.bfloat16)


def level_of(stream_key, extent, cuts, smallest, top_value):
    gain = 1.0
    for dim, shards_of in cuts:
        steps = jax.random.uniform(jax.random.fold_in(jax.random.fold_in(stream_key, 6), dim), (shards_of,), jnp.float32, smallest / len(cuts), top_value / len(cuts))
        gain = gain * jnp.repeat(jnp.exp(steps), extent[dim] // shards_of).reshape((-1,) + (1,) * (len(extent) - 1 - dim))
    return gain


def bell_draw(rng, extent, deviation, most, cuts=(), kind=jnp.bfloat16):
    level = level_of(rng, extent, cuts, -0.22, 0.18) if cuts else 1.0
    entries = jax.random.normal(rng, extent, jnp.float32) * deviation * level
    return jnp.minimum(jnp.maximum(entries, -most), most).astype(kind)


def setup_inputs(seed: int = 0) -> dict:
    arg_keys = jax.random.split(jax.random.key(seed), 5)
    stream = draw_stream(jax.random.fold_in(arg_keys[4], 71), 0)
    score_scale = draw_score_scale(jax.random.fold_in(arg_keys[4], 71), 0)
    value_weight = bell_draw(arg_keys[2], (SECTIONS, D, D), D ** -0.5, 0.125, ((0, 4), (2, 4)))
    out_weight = bell_draw(arg_keys[3], (SECTIONS, D, D), (D // 4) ** -0.5, 0.25, ((0, 4), (1, 4)))
    return {"stream": stream, "score_scale": score_scale, "value_weight": value_weight, "out_weight": out_weight}


def attend_all(normed, query_scale, value_matrix):
    window_count = COLS // WIN
    token_count = ROWS * WIN
    normed_f = normed.astype(jnp.float32)
    queries = lax.optimization_barrier((normed_f * query_scale).astype(jnp.bfloat16))
    values = jnp.dot(normed.reshape(ROWS * COLS, D), value_matrix, preferred_element_type=jnp.float32)
    values = lax.optimization_barrier(values.astype(jnp.bfloat16)).reshape(ROWS, COLS, D)
    inv_root = 1.0 / math.sqrt(HEAD_DIM)

    def one_window(window_id):
        first_col = (window_id * WIN).astype(jnp.int32)

        def take_window(tensor):
            window_part = lax.dynamic_slice_in_dim(tensor, first_col, WIN, 1)
            return window_part.reshape(token_count, HEADS, HEAD_DIM).astype(jnp.float32)
        scores = jnp.einsum('qhd,khd->hqk', take_window(queries), take_window(normed)) * inv_root
        attention_probabilities = jax.nn.softmax(scores, axis=-1)
        attention_probabilities = lax.optimization_barrier(attention_probabilities.astype(jnp.bfloat16)).astype(jnp.float32)
        attended = jnp.einsum('hqk,khd->qhd', attention_probabilities, take_window(values))
        return attended.astype(jnp.bfloat16).reshape(ROWS, WIN, D)
    results = lax.map(one_window, jnp.arange(window_count, dtype=jnp.int32))
    return results.transpose(1, 0, 2, 3).reshape(ROWS, COLS, D)

def project_out(attended, out_matrix):
    flattened = attended.reshape(ROWS * COLS, D)
    group_width = D // N_HEAD
    exponent_total = jnp.zeros((ROWS * COLS, D), jnp.float32)
    for group_index in range(N_HEAD):
        lower = group_index * group_width
        piece_term = jnp.dot(flattened[:, lower:lower + group_width], out_matrix[lower:lower + group_width], preferred_element_type=jnp.float32)
        exponent_total = exponent_total + lax.optimization_barrier(piece_term.astype(jnp.bfloat16)).astype(jnp.float32)
    return exponent_total.reshape(ROWS, COLS, D)

def reference(stream, score_scale, value_weight, out_weight):
    current = stream
    collected = []
    for section in range(SECTIONS):
        current_f = current.astype(jnp.float32)
        mean_square = lax.optimization_barrier(jnp.mean(current_f * current_f, axis=2, keepdims=True))
        normed = lax.optimization_barrier((current_f * lax.rsqrt(mean_square + 1e-06)).astype(jnp.bfloat16))
        offset_cols = section % 2 * (WIN // 2)
        aligned = jnp.roll(normed, -offset_cols, axis=1)
        attended = attend_all(aligned, score_scale[section], value_weight[section])
        attended = jnp.roll(attended, offset_cols, axis=1)
        mixture = project_out(attended, out_weight[section])
        updated = (current_f + mixture).astype(jnp.bfloat16)
        current = lax.optimization_barrier(updated)
        collected.append(current)
    return jnp.stack(collected)
```

```python
import functools
import math

import jax
import jax.numpy as jnp
from jax import lax
from jax.experimental import pallas as pl
from jax.experimental.pallas import tpu as pltpu
from jax.sharding import PartitionSpec as P

MESH = pl.DeviceIdType.MESH
HEAD_DIM = 128
EPSILON = 1e-06
BF16, F32 = jnp.bfloat16, jnp.float32

CHUNKS = 4
RIGHT, LEFT = 0, 1


def kernel(
    sizes, stream, scale, wv_hbm, wo_hbm, out,
    xin, wv, wo, ubuf, vbuf, obuf, g2, r2, gown, gside, gsend, grecv, xnew,
    w_sem, own_sem, ag_s, ag_r, rl_s, rl_r, r2_s, r2_r, rs_s, rs_r, pp_s, pp_r, os_s, os_r, out_sem,
):
    n_pipe, n_win, n_head = sizes
    rows, half_cols, width = xin.shape[1:]
    cut = width // n_head
    heads = cut // HEAD_DIM
    per_half = CHUNKS // 2
    crows = rows // per_half
    cells = crows * half_cols
    my_rows = stream.shape[0]
    p, w, h = lax.axis_index("pipe"), lax.axis_index("win"), lax.axis_index("head")
    odd = lax.rem(p, 2)
    right, left, far = lax.rem(h + 1, n_head), lax.rem(h + n_head - 1, n_head), lax.rem(h + 2, n_head)
    w_next, w_prev = lax.rem(w + 1, n_win), lax.rem(w + n_win - 1, n_win)
    w_to = lax.rem(w + n_win - 1 + 2 * odd, n_win)
    w_from = lax.rem(w + n_win - 1 + 2 * odd, n_win)
    side = ((p, w, right), (p, w, left))

    def lanes(k):
        return pl.ds(pl.multiple_of(k * cut, cut), cut)

    def remote(src, dst, s_sem, r_sem, to):
        return pltpu.make_async_remote_copy(
            src_ref=src, dst_ref=dst, send_sem=s_sem, recv_sem=r_sem, device_id=to, device_id_type=MESH)

    load_v = pltpu.make_async_copy(wv_hbm.at[0], wv, w_sem.at[0])
    load_o = pltpu.make_async_copy(wo_hbm.at[0], wo, w_sem.at[1])

    barrier = pltpu.get_barrier_semaphore()

    def greet(to):
        pl.semaphore_signal(barrier, inc=1, device_id=to, device_id_type=MESH)

    greet(side[RIGHT])
    greet(side[LEFT])

    @pl.when(p > 0)
    def _():
        greet((p - 1, w, h))
        greet((p - 1, w_from, h))

    @pl.when(odd == 1)
    def _():
        greet((p, w_prev, h))

    @pl.when(p > 0)
    def _():
        load_v.start()
        load_o.start()

    for k in range(n_pipe):
        @pl.when(p == k)
        def _():
            pl.semaphore_wait(barrier, 2 + 2 * (k < n_pipe - 1) + k % 2)

    def place(c):
        return c // per_half, (c % per_half) * crows

    def normalize(c):
        a, r0 = place(c)
        x = xin[a, r0:r0 + crows].reshape(cells, width).astype(F32)
        inverse = lax.rsqrt(jnp.sum(x * x, axis=1, keepdims=True) * (1.0 / width) + EPSILON)
        u = (x * inverse).astype(BF16)
        mine = xin[a, r0:r0 + crows, :, lanes(h)].reshape(cells, cut).astype(F32)
        ubuf[c * cells:(c + 1) * cells, :] = (mine * inverse).astype(BF16)
        vbuf[c * cells:(c + 1) * cells, :] = jnp.dot(u, wv[...], preferred_element_type=F32).astype(BF16)

    @pl.when(p == 0)
    def _():
        def rows_of(k):
            return pl.ds(k * my_rows, my_rows)

        def spread(a, d):
            return remote(
                stream.at[:, pl.ds(a * half_cols, half_cols)], xin.at[a, rows_of(h)],
                ag_s.at[d, a], ag_r.at[d, a], side[d])

        def relay(a, d):
            row = (left if d == RIGHT else right) * my_rows + d
            part = xin.at[a, pl.ds(row, 1)]
            return remote(part, part, rl_s.at[d, a], rl_r.at[d, a], side[d])

        own = [
            pltpu.make_async_copy(
                stream.at[:, pl.ds(a * half_cols, half_cols)], xin.at[a, rows_of(h)], own_sem.at[a])
            for a in range(2)
        ]
        for a in range(2):
            for d in (RIGHT, LEFT):
                spread(a, d).start()
            own[a].start()
        load_v.start()
        load_o.start()
        for a in range(2):
            for d in (RIGHT, LEFT):
                spread(a, d).wait_recv()
                relay(a, d).start()
        load_v.wait()
        for a in range(2):
            own[a].wait()
            for d in (RIGHT, LEFT):
                relay(a, d).wait_recv()
            for c in range(a * per_half, (a + 1) * per_half):
                normalize(c)
        for a in range(2):
            for d in (RIGHT, LEFT):
                spread(a, d).wait_send()
                relay(a, d).wait_send()

    def hand_on(c):
        a, r0 = place(c)
        to = (p + 1, w_to if a == 0 else w, h)
        return remote(
            xnew.at[a, pl.ds(r0, crows)], xin.at[a, pl.ds(r0, crows), :, lanes(h)],
            pp_s.at[c], pp_r.at[c], to)

    @pl.when(p > 0)
    def _():
        def spread(c, d):
            a, r0 = place(c)
            part = xin.at[a, pl.ds(r0, crows), :, lanes(h)]
            return remote(part, part, ag_s.at[d, c], ag_r.at[d, c], side[d])

        def relay(c, d):
            a, r0 = place(c)
            part = xin.at[a, pl.ds(r0 + d * (crows // 2), crows // 2), :, lanes(left if d == RIGHT else right)]
            return remote(part, part, rl_s.at[d, c], rl_r.at[d, c], side[d])

        load_v.wait()
        for i in range(CHUNKS + 2):
            if i < CHUNKS:
                hand_on(i).wait_recv()
                for d in (RIGHT, LEFT):
                    spread(i, d).start()
            if 1 <= i <= CHUNKS:
                for d in (RIGHT, LEFT):
                    spread(i - 1, d).wait_recv()
                    relay(i - 1, d).start()
            if i >= 2:
                for d in (RIGHT, LEFT):
                    relay(i - 2, d).wait_recv()
                normalize(i - 2)
        for c in range(CHUNKS):
            for d in (RIGHT, LEFT):
                spread(c, d).wait_send()
                relay(c, d).wait_send()

    load_o.wait()
    inv_root = 1.0 / math.sqrt(HEAD_DIM)

    def attend(c):
        for j in range(heads):
            col = slice(j * HEAD_DIM, (j + 1) * HEAD_DIM)
            gain = scale[:, pl.ds(pl.multiple_of(h * cut + j * HEAD_DIM, HEAD_DIM), HEAD_DIM)]
            q = (ubuf[c * cells:(c + 1) * cells, col].astype(F32) * gain).astype(BF16)
            s = lax.dot_general(q, ubuf[:, col], (((1,), (1,)), ((), ())), preferred_element_type=F32) * inv_root
            e = jnp.exp(s - jnp.max(s, axis=1, keepdims=True))
            prob = (e / jnp.sum(e, axis=1, keepdims=True)).astype(BF16)
            obuf[c, :, col] = jnp.dot(prob, vbuf[:, col], preferred_element_type=F32).astype(BF16)

    def project(c, k):
        return jnp.dot(obuf[c], wo[:, lanes(k)], preferred_element_type=F32)

    half_cells = cells // 2

    def far_share(c, d):
        rows_ = pl.ds(d * half_cells, half_cells)
        return remote(g2.at[c, rows_], r2.at[c, d], r2_s.at[d, c], r2_r.at[d, c], side[d])

    def near_share(c, d):
        return remote(gsend.at[c, d], grecv.at[c, d], rs_s.at[d, c], rs_r.at[d, c], side[d])

    def cols_of(a):
        return pl.ds(a * half_cols, half_cols)

    def keep(c):
        a, r0 = place(c)
        return pltpu.make_async_copy(
            xnew.at[a, pl.ds(r0, crows)], out.at[0, pl.ds(r0, crows), cols_of(a)], out_sem.at[c])

    def keep_next(c):
        a, r0 = place(c)
        return remote(
            xnew.at[a, pl.ds(r0, crows)], out.at[0, pl.ds(r0, crows), cols_of(a)],
            os_s.at[c], os_r.at[c], (p, w_next, h))

    for i in range(CHUNKS + 2):
        if i < CHUNKS:
            c = i
            attend(c)
            g2[c] = project(c, far).astype(BF16)
            for d in (RIGHT, LEFT):
                far_share(c, d).start()
            gside[c, RIGHT] = project(c, right)
            gside[c, LEFT] = project(c, left)
            gown[c] = project(c, h)
        if 1 <= i <= CHUNKS:
            c = i - 1
            for d in (RIGHT, LEFT):
                far_share(c, d).wait_recv()
                first = d * half_cells
                rest = (1 - d) * half_cells
                gsend[c, d, first:first + half_cells] = (
                    gside[c, d, first:first + half_cells] + r2[c, d].astype(F32)).astype(BF16)
                gsend[c, d, rest:rest + half_cells] = gside[c, d, rest:rest + half_cells].astype(BF16)
                near_share(c, d).start()
        if i >= 2:
            c = i - 2
            a, r0 = place(c)
            total = xin[a, r0:r0 + crows, :, lanes(h)].reshape(cells, cut).astype(F32) + gown[c]
            for d in (RIGHT, LEFT):
                near_share(c, d).wait_recv()
                total = total + grecv[c, d].astype(F32)
            xnew[a, r0:r0 + crows] = total.astype(BF16).reshape(crows, half_cols, cut)

            @pl.when(p < n_pipe - 1)
            def _():
                hand_on(c).start()

            if a == 1:
                keep(c).start()
            else:
                @pl.when(odd == 0)
                def _():
                    keep(c).start()

                @pl.when(odd == 1)
                def _():
                    keep_next(c).start()

    for c in range(CHUNKS):
        for d in (RIGHT, LEFT):
            far_share(c, d).wait_send()
            near_share(c, d).wait_send()

        @pl.when(p < n_pipe - 1)
        def _():
            hand_on(c).wait_send()

        if place(c)[0] == 1:
            keep(c).wait()
        else:
            @pl.when(odd == 0)
            def _():
                keep(c).wait()

            @pl.when(odd == 1)
            def _():
                keep_next(c).wait_send()
                keep_next(c).wait_recv()


def solution(mesh):
    sizes = tuple(mesh.shape[name] for name in ("pipe", "win", "head"))

    def per_device(stream, score_scale, value_weight, out_weight):
        my_rows, cols, width = stream.shape
        rows, half_cols, cut = my_rows * sizes[2], cols // 2, width // sizes[2]
        cells = rows * cols // CHUNKS
        anywhere = pl.BlockSpec(memory_space=pl.ANY)
        dma = pltpu.SemaphoreType.DMA
        return pl.pallas_call(
            functools.partial(kernel, sizes),
            out_shape=jax.ShapeDtypeStruct((1, rows, cols, cut), BF16),
            in_specs=[anywhere, pl.BlockSpec(memory_space=pltpu.VMEM), anywhere, anywhere],
            out_specs=anywhere,
            scratch_shapes=[
                pltpu.VMEM((2, rows, half_cols, width), BF16),
                pltpu.VMEM((width, cut), BF16),
                pltpu.VMEM((cut, width), BF16),
                pltpu.VMEM((rows * cols, cut), BF16),
                pltpu.VMEM((rows * cols, cut), BF16),
                pltpu.VMEM((CHUNKS, cells, cut), BF16),
                pltpu.VMEM((CHUNKS, cells, cut), BF16),
                pltpu.VMEM((CHUNKS, 2, cells // 2, cut), BF16),
                pltpu.VMEM((CHUNKS, cells, cut), F32),
                pltpu.VMEM((CHUNKS, 2, cells, cut), F32),
                pltpu.VMEM((CHUNKS, 2, cells, cut), BF16),
                pltpu.VMEM((CHUNKS, 2, cells, cut), BF16),
                pltpu.VMEM((2, rows, half_cols, cut), BF16),
                dma((2,)), dma((2,)),
                dma((2, CHUNKS)), dma((2, CHUNKS)),
                dma((2, CHUNKS)), dma((2, CHUNKS)),
                dma((2, CHUNKS)), dma((2, CHUNKS)),
                dma((2, CHUNKS)), dma((2, CHUNKS)),
                dma((CHUNKS,)), dma((CHUNKS,)),
                dma((CHUNKS,)), dma((CHUNKS,)),
                dma((CHUNKS,)),
            ],
            compiler_params=pltpu.CompilerParams(collective_id=0, has_side_effects=True),
        )(stream, score_scale, value_weight, out_weight)

    return jax.shard_map(
        per_device,
        mesh=mesh,
        in_specs=(P("head", "win", None), P("pipe", None), P("pipe", None, "head"), P("pipe", "head", None)),
        out_specs=P("pipe", None, "win", "head"),
        check_vma=False,
    )
```

```python
import functools
import math

import jax
import jax.numpy as jnp
from jax import lax
from jax.experimental import pallas as pl
from jax.experimental.pallas import tpu as pltpu
from jax.sharding import PartitionSpec as P

MESH = pl.DeviceIdType.MESH
HEAD_DIM = 128
EPSILON = 1e-06
BF16, F32 = jnp.bfloat16, jnp.float32

CHUNKS = 8
RIGHT, LEFT = 0, 1


def kernel(
    sizes, stream, scale, wv_hbm, wo_hbm, out,
    xin, wv, wo, ubuf, vbuf, obuf, g2, r2, gown, gside, gsend, grecv, xnew,
    w_sem, own_sem, ag_s, ag_r, rl_s, rl_r, r2_s, r2_r, rs_s, rs_r, pp_s, pp_r, os_s, os_r, out_sem,
):
    n_pipe, n_win, n_head = sizes
    rows, half_cols, width = xin.shape[1:]
    cut = width // n_head
    heads = cut // HEAD_DIM
    per_half = CHUNKS // 2
    crows = rows // per_half
    cells = crows * half_cols
    my_rows = stream.shape[0]
    p, w, h = lax.axis_index("pipe"), lax.axis_index("win"), lax.axis_index("head")
    odd = lax.rem(p, 2)
    right, left, far = lax.rem(h + 1, n_head), lax.rem(h + n_head - 1, n_head), lax.rem(h + 2, n_head)
    w_next, w_prev = lax.rem(w + 1, n_win), lax.rem(w + n_win - 1, n_win)
    w_to = lax.rem(w + n_win - 1 + 2 * odd, n_win)
    w_from = lax.rem(w + n_win - 1 + 2 * odd, n_win)
    side = ((p, w, right), (p, w, left))

    def lanes(k):
        return pl.ds(pl.multiple_of(k * cut, cut), cut)

    def remote(src, dst, s_sem, r_sem, to):
        return pltpu.make_async_remote_copy(
            src_ref=src, dst_ref=dst, send_sem=s_sem, recv_sem=r_sem, device_id=to, device_id_type=MESH)

    load_v = pltpu.make_async_copy(wv_hbm.at[0], wv, w_sem.at[0])
    load_o = pltpu.make_async_copy(wo_hbm.at[0], wo, w_sem.at[1])

    barrier = pltpu.get_barrier_semaphore()

    def greet(to):
        pl.semaphore_signal(barrier, inc=1, device_id=to, device_id_type=MESH)

    greet(side[RIGHT])
    greet(side[LEFT])

    @pl.when(p > 0)
    def _():
        greet((p - 1, w, h))
        greet((p - 1, w_from, h))

    @pl.when(odd == 1)
    def _():
        greet((p, w_prev, h))

    @pl.when(p > 0)
    def _():
        load_v.start()
        load_o.start()

    for k in range(n_pipe):
        @pl.when(p == k)
        def _():
            pl.semaphore_wait(barrier, 2 + 2 * (k < n_pipe - 1) + k % 2)

    def place(c):
        return c // per_half, (c % per_half) * crows

    def normalize(c):
        a, r0 = place(c)
        x = xin[a, r0:r0 + crows].reshape(cells, width).astype(F32)
        inverse = lax.rsqrt(jnp.sum(x * x, axis=1, keepdims=True) * (1.0 / width) + EPSILON)
        u = (x * inverse).astype(BF16)
        mine = xin[a, r0:r0 + crows, :, lanes(h)].reshape(cells, cut).astype(F32)
        ubuf[c * cells:(c + 1) * cells, :] = (mine * inverse).astype(BF16)
        vbuf[c * cells:(c + 1) * cells, :] = jnp.dot(u, wv[...], preferred_element_type=F32).astype(BF16)

    @pl.when(p == 0)
    def _():
        def rows_of(k):
            return pl.ds(k * my_rows, my_rows)

        def spread(a, d):
            return remote(
                stream.at[:, pl.ds(a * half_cols, half_cols)], xin.at[a, rows_of(h)],
                ag_s.at[d, a], ag_r.at[d, a], side[d])

        def relay(a, d):
            row = (left if d == RIGHT else right) * my_rows + d
            part = xin.at[a, pl.ds(row, 1)]
            return remote(part, part, rl_s.at[d, a], rl_r.at[d, a], side[d])

        own = [
            pltpu.make_async_copy(
                stream.at[:, pl.ds(a * half_cols, half_cols)], xin.at[a, rows_of(h)], own_sem.at[a])
            for a in range(2)
        ]
        for a in range(2):
            for d in (RIGHT, LEFT):
                spread(a, d).start()
            own[a].start()
        load_v.start()
        load_o.start()
        for a in range(2):
            for d in (RIGHT, LEFT):
                spread(a, d).wait_recv()
                relay(a, d).start()
        load_v.wait()
        for a in range(2):
            own[a].wait()
            for d in (RIGHT, LEFT):
                relay(a, d).wait_recv()
            for c in range(a * per_half, (a + 1) * per_half):
                normalize(c)
        for a in range(2):
            for d in (RIGHT, LEFT):
                spread(a, d).wait_send()
                relay(a, d).wait_send()

    def hand_on(c):
        a, r0 = place(c)
        to = (p + 1, w_to if a == 0 else w, h)
        return remote(
            xnew.at[a, pl.ds(r0, crows)], xin.at[a, pl.ds(r0, crows), :, lanes(h)],
            pp_s.at[c], pp_r.at[c], to)

    @pl.when(p > 0)
    def _():
        def spread(c, d):
            a, r0 = place(c)
            part = xin.at[a, pl.ds(r0, crows), :, lanes(h)]
            return remote(part, part, ag_s.at[d, c], ag_r.at[d, c], side[d])

        def relay(c, d):
            a, r0 = place(c)
            part = xin.at[a, pl.ds(r0 + d * (crows // 2), crows // 2), :, lanes(left if d == RIGHT else right)]
            return remote(part, part, rl_s.at[d, c], rl_r.at[d, c], side[d])

        load_v.wait()
        for i in range(CHUNKS + 2):
            if i < CHUNKS:
                hand_on(i).wait_recv()
                for d in (RIGHT, LEFT):
                    spread(i, d).start()
            if 1 <= i <= CHUNKS:
                for d in (RIGHT, LEFT):
                    spread(i - 1, d).wait_recv()
                    relay(i - 1, d).start()
            if i >= 2:
                for d in (RIGHT, LEFT):
                    relay(i - 2, d).wait_recv()
                normalize(i - 2)
        for c in range(CHUNKS):
            for d in (RIGHT, LEFT):
                spread(c, d).wait_send()
                relay(c, d).wait_send()

    load_o.wait()
    inv_root = 1.0 / math.sqrt(HEAD_DIM)

    def attend(c):
        for j in range(heads):
            col = slice(j * HEAD_DIM, (j + 1) * HEAD_DIM)
            gain = scale[:, pl.ds(pl.multiple_of(h * cut + j * HEAD_DIM, HEAD_DIM), HEAD_DIM)]
            q = (ubuf[c * cells:(c + 1) * cells, col].astype(F32) * gain).astype(BF16)
            s = lax.dot_general(q, ubuf[:, col], (((1,), (1,)), ((), ())), preferred_element_type=F32) * inv_root
            e = jnp.exp(s - jnp.max(s, axis=1, keepdims=True))
            prob = (e / jnp.sum(e, axis=1, keepdims=True)).astype(BF16)
            obuf[c, :, col] = jnp.dot(prob, vbuf[:, col], preferred_element_type=F32).astype(BF16)

    def project(c, k):
        return jnp.dot(obuf[c], wo[:, lanes(k)], preferred_element_type=F32)

    half_cells = cells // 2

    def far_share(c, d):
        rows_ = pl.ds(d * half_cells, half_cells)
        return remote(g2.at[c, rows_], r2.at[c, d], r2_s.at[d, c], r2_r.at[d, c], side[d])

    def near_share(c, d):
        return remote(gsend.at[c, d], grecv.at[c, d], rs_s.at[d, c], rs_r.at[d, c], side[d])

    def cols_of(a):
        return pl.ds(a * half_cols, half_cols)

    def keep(c):
        a, r0 = place(c)
        return pltpu.make_async_copy(
            xnew.at[a, pl.ds(r0, crows)], out.at[0, pl.ds(r0, crows), cols_of(a)], out_sem.at[c])

    def keep_next(c):
        a, r0 = place(c)
        return remote(
            xnew.at[a, pl.ds(r0, crows)], out.at[0, pl.ds(r0, crows), cols_of(a)],
            os_s.at[c], os_r.at[c], (p, w_next, h))

    for i in range(CHUNKS + 2):
        if i < CHUNKS:
            c = i
            attend(c)
            g2[c] = project(c, far).astype(BF16)
            for d in (RIGHT, LEFT):
                far_share(c, d).start()
            gside[c, RIGHT] = project(c, right)
            gside[c, LEFT] = project(c, left)
            gown[c] = project(c, h)
        if 1 <= i <= CHUNKS:
            c = i - 1
            for d in (RIGHT, LEFT):
                far_share(c, d).wait_recv()
                first = d * half_cells
                rest = (1 - d) * half_cells
                gsend[c, d, first:first + half_cells] = (
                    gside[c, d, first:first + half_cells] + r2[c, d].astype(F32)).astype(BF16)
                gsend[c, d, rest:rest + half_cells] = gside[c, d, rest:rest + half_cells].astype(BF16)
                near_share(c, d).start()
        if i >= 2:
            c = i - 2
            a, r0 = place(c)
            total = xin[a, r0:r0 + crows, :, lanes(h)].reshape(cells, cut).astype(F32) + gown[c]
            for d in (RIGHT, LEFT):
                near_share(c, d).wait_recv()
                total = total + grecv[c, d].astype(F32)
            xnew[a, r0:r0 + crows] = total.astype(BF16).reshape(crows, half_cols, cut)

            @pl.when(p < n_pipe - 1)
            def _():
                hand_on(c).start()

            if a == 1:
                keep(c).start()
            else:
                @pl.when(odd == 0)
                def _():
                    keep(c).start()

                @pl.when(odd == 1)
                def _():
                    keep_next(c).start()

    for c in range(CHUNKS):
        for d in (RIGHT, LEFT):
            far_share(c, d).wait_send()
            near_share(c, d).wait_send()

        @pl.when(p < n_pipe - 1)
        def _():
            hand_on(c).wait_send()

        if place(c)[0] == 1:
            keep(c).wait()
        else:
            @pl.when(odd == 0)
            def _():
                keep(c).wait()

            @pl.when(odd == 1)
            def _():
                keep_next(c).wait_send()
                keep_next(c).wait_recv()


def solution(mesh):
    sizes = tuple(mesh.shape[name] for name in ("pipe", "win", "head"))

    def per_device(stream, score_scale, value_weight, out_weight):
        my_rows, cols, width = stream.shape
        rows, half_cols, cut = my_rows * sizes[2], cols // 2, width // sizes[2]
        cells = rows * cols // CHUNKS
        anywhere = pl.BlockSpec(memory_space=pl.ANY)
        dma = pltpu.SemaphoreType.DMA
        return pl.pallas_call(
            functools.partial(kernel, sizes),
            out_shape=jax.ShapeDtypeStruct((1, rows, cols, cut), BF16),
            in_specs=[anywhere, pl.BlockSpec(memory_space=pltpu.VMEM), anywhere, anywhere],
            out_specs=anywhere,
            scratch_shapes=[
                pltpu.VMEM((2, rows, half_cols, width), BF16),
                pltpu.VMEM((width, cut), BF16),
                pltpu.VMEM((cut, width), BF16),
                pltpu.VMEM((rows * cols, cut), BF16),
                pltpu.VMEM((rows * cols, cut), BF16),
                pltpu.VMEM((CHUNKS, cells, cut), BF16),
                pltpu.VMEM((CHUNKS, cells, cut), BF16),
                pltpu.VMEM((CHUNKS, 2, cells // 2, cut), BF16),
                pltpu.VMEM((CHUNKS, cells, cut), F32),
                pltpu.VMEM((CHUNKS, 2, cells, cut), F32),
                pltpu.VMEM((CHUNKS, 2, cells, cut), BF16),
                pltpu.VMEM((CHUNKS, 2, cells, cut), BF16),
                pltpu.VMEM((2, rows, half_cols, cut), BF16),
                dma((2,)), dma((2,)),
                dma((2, CHUNKS)), dma((2, CHUNKS)),
                dma((2, CHUNKS)), dma((2, CHUNKS)),
                dma((2, CHUNKS)), dma((2, CHUNKS)),
                dma((2, CHUNKS)), dma((2, CHUNKS)),
                dma((CHUNKS,)), dma((CHUNKS,)),
                dma((CHUNKS,)), dma((CHUNKS,)),
                dma((CHUNKS,)),
            ],
            compiler_params=pltpu.CompilerParams(collective_id=0, has_side_effects=True),
        )(stream, score_scale, value_weight, out_weight)

    return jax.shard_map(
        per_device,
        mesh=mesh,
        in_specs=(P("head", "win", None), P("pipe", None), P("pipe", None, "head"), P("pipe", "head", None)),
        out_specs=P("pipe", None, "win", "head"),
        check_vma=False,
    )
```

```python
import functools
import math

import jax
import jax.numpy as jnp
from jax import lax
from jax.experimental import pallas as pl
from jax.experimental.pallas import tpu as pltpu
from jax.sharding import PartitionSpec as P

MESH = pl.DeviceIdType.MESH
HEAD_DIM = 128
EPSILON = 1e-06
BF16, F32 = jnp.bfloat16, jnp.float32

CHUNKS = ((0, 0, 1), (0, 1, 2), (0, 3, 2), (0, 5, 3), (1, 0, 3), (1, 3, 2), (1, 5, 2), (1, 7, 1))
COUNT = len(CHUNKS)
FIRST_OF_1 = next(c for c in range(COUNT) if CHUNKS[c][0] == 1)
RIGHT, LEFT = 0, 1


def kernel(
    sizes, stream, scale, wv_hbm, wo_hbm, out,
    xin, wv, wo, ubuf, vbuf, obuf, g2, r2, rfar, gown, gside, gsend, grecv, xnew,
    w_sem, own_sem, ag_s, ag_r, rl_s, rl_r, r2_s, r2_r, rs_s, rs_r, pp_s, pp_r, os_s, os_r, out_sem,
):
    n_pipe, n_win, n_head = sizes
    rows, half_cols, width = xin.shape[1:]
    cut = width // n_head
    half_cut = cut // 2
    heads = cut // HEAD_DIM
    half = rows * half_cols
    my_rows = stream.shape[0]
    p, w, h = lax.axis_index("pipe"), lax.axis_index("win"), lax.axis_index("head")
    odd = lax.rem(p, 2)
    right, left, far = lax.rem(h + 1, n_head), lax.rem(h + n_head - 1, n_head), lax.rem(h + 2, n_head)
    w_next, w_prev = lax.rem(w + 1, n_win), lax.rem(w + n_win - 1, n_win)
    w_to = lax.rem(w + n_win - 1 + 2 * odd, n_win)
    w_from = lax.rem(w + n_win - 1 + 2 * odd, n_win)
    side = ((p, w, right), (p, w, left))
    across = (p, w, far)

    def lanes(k):
        return pl.ds(pl.multiple_of(k * cut, cut), cut)

    def half_lanes(k, d):
        return pl.ds(pl.multiple_of(k * cut + d * half_cut, half_cut), half_cut)

    def remote(src, dst, s_sem, r_sem, to):
        return pltpu.make_async_remote_copy(
            src_ref=src, dst_ref=dst, send_sem=s_sem, recv_sem=r_sem, device_id=to, device_id_type=MESH)

    load_v = pltpu.make_async_copy(wv_hbm.at[0], wv, w_sem.at[0])
    load_o = pltpu.make_async_copy(wo_hbm.at[0], wo, w_sem.at[1])

    barrier = pltpu.get_barrier_semaphore()

    def greet(to):
        pl.semaphore_signal(barrier, inc=1, device_id=to, device_id_type=MESH)

    greet(side[RIGHT])
    greet(side[LEFT])
    greet(across)

    @pl.when(p > 0)
    def _():
        greet((p - 1, w, h))
        greet((p - 1, w_from, h))

    @pl.when(odd == 1)
    def _():
        greet((p, w_prev, h))

    @pl.when(p > 0)
    def _():
        load_v.start()
        load_o.start()

    for k in range(n_pipe):
        @pl.when(p == k)
        def _():
            pl.semaphore_wait(barrier, 3 + 2 * (k < n_pipe - 1) + k % 2)

    def span(c):
        a, r0, nr = CHUNKS[c]
        return a * half + r0 * half_cols, nr * half_cols

    def direct_sum(c):
        return c == 0

    def direct_gather(c):
        return c == COUNT - 1

    def normalize(a):
        x = xin[a].reshape(half, width).astype(F32)
        inverse = lax.rsqrt(jnp.sum(x * x, axis=1, keepdims=True) * (1.0 / width) + EPSILON)
        u = (x * inverse).astype(BF16)
        mine = xin[a, :, :, lanes(h)].reshape(half, cut).astype(F32)
        ubuf[a * half:(a + 1) * half, :] = (mine * inverse).astype(BF16)
        vbuf[a * half:(a + 1) * half, :] = jnp.dot(u, wv[...], preferred_element_type=F32).astype(BF16)

    @pl.when(p == 0)
    def _():
        def rows_of(k):
            return pl.ds(k * my_rows, my_rows)

        def spread(a, d):
            return remote(
                stream.at[:, pl.ds(a * half_cols, half_cols)], xin.at[a, rows_of(h)],
                ag_s.at[d, a], ag_r.at[d, a], side[d])

        def relay(a, d):
            row = (left if d == RIGHT else right) * my_rows + d
            part = xin.at[a, pl.ds(row, 1)]
            return remote(part, part, rl_s.at[d, a], rl_r.at[d, a], side[d])

        own = [
            pltpu.make_async_copy(
                stream.at[:, pl.ds(a * half_cols, half_cols)], xin.at[a, rows_of(h)], own_sem.at[a])
            for a in range(2)
        ]
        for a in range(2):
            for d in (RIGHT, LEFT):
                spread(a, d).start()
            own[a].start()
        load_v.start()
        load_o.start()
        for a in range(2):
            for d in (RIGHT, LEFT):
                spread(a, d).wait_recv()
                relay(a, d).start()
        load_v.wait()
        for a in range(2):
            own[a].wait()
            for d in (RIGHT, LEFT):
                relay(a, d).wait_recv()
            normalize(a)
        for a in range(2):
            for d in (RIGHT, LEFT):
                spread(a, d).wait_send()
                relay(a, d).wait_send()

    def hand_on(c):
        a, r0, nr = CHUNKS[c]
        to = (p + 1, w_to if a == 0 else w, h)
        return remote(
            xnew.at[a, pl.ds(r0, nr)], xin.at[a, pl.ds(r0, nr), :, lanes(h)],
            pp_s.at[c], pp_r.at[c], to)

    @pl.when(p > 0)
    def _():
        def spread(c, d):
            a, r0, nr = CHUNKS[c]
            part = xin.at[a, pl.ds(r0, nr), :, lanes(h)]
            return remote(part, part, ag_s.at[d, c], ag_r.at[d, c], side[d])

        def relays(c):
            a, r0, nr = CHUNKS[c]
            if direct_gather(c):
                part = xin.at[a, pl.ds(r0, nr), :, lanes(h)]
                return [remote(part, part, rl_s.at[0, c], rl_r.at[0, c], across)]
            made = []
            for d in (RIGHT, LEFT):
                part = xin.at[a, pl.ds(r0, nr), :, half_lanes(left if d == RIGHT else right, d)]
                made.append(remote(part, part, rl_s.at[d, c], rl_r.at[d, c], side[d]))
            return made

        load_v.wait()
        for i in range(COUNT + 2):
            if i < COUNT:
                hand_on(i).wait_recv()
                for d in (RIGHT, LEFT):
                    spread(i, d).start()
                if direct_gather(i):
                    relays(i)[0].start()
            if 1 <= i <= COUNT:
                for d in (RIGHT, LEFT):
                    spread(i - 1, d).wait_recv()
                    if not direct_gather(i - 1):
                        relays(i - 1)[d].start()
            if i >= 2:
                for copy in relays(i - 2):
                    copy.wait_recv()
                if i - 2 == FIRST_OF_1 - 1:
                    normalize(0)
        normalize(1)
        for c in range(COUNT):
            for d in (RIGHT, LEFT):
                spread(c, d).wait_send()
            for copy in relays(c):
                copy.wait_send()

    load_o.wait()
    inv_root = 1.0 / math.sqrt(HEAD_DIM)

    def attend(a):
        for j in range(heads):
            col = slice(j * HEAD_DIM, (j + 1) * HEAD_DIM)
            gain = scale[:, pl.ds(pl.multiple_of(h * cut + j * HEAD_DIM, HEAD_DIM), HEAD_DIM)]
            q = (ubuf[a * half:(a + 1) * half, col].astype(F32) * gain).astype(BF16)
            s = lax.dot_general(q, ubuf[:, col], (((1,), (1,)), ((), ())), preferred_element_type=F32) * inv_root
            e = jnp.exp(s - jnp.max(s, axis=1, keepdims=True))
            prob = (e / jnp.sum(e, axis=1, keepdims=True)).astype(BF16)
            obuf[a, :, col] = jnp.dot(prob, vbuf[:, col], preferred_element_type=F32).astype(BF16)

    def project(a, k):
        return jnp.dot(obuf[a], wo[:, lanes(k)], preferred_element_type=F32)

    def far_shares(c):
        t0, n = span(c)
        if direct_sum(c):
            return [remote(g2.at[pl.ds(t0, n)], rfar, r2_s.at[0, c], r2_r.at[0, c], across)]
        return [
            remote(g2.at[pl.ds(t0, n), pl.ds(d * half_cut, half_cut)], r2.at[d, pl.ds(t0, n)],
                   r2_s.at[d, c], r2_r.at[d, c], side[d])
            for d in (RIGHT, LEFT)
        ]

    def near_share(c, d):
        t0, n = span(c)
        return remote(gsend.at[d, pl.ds(t0, n)], grecv.at[d, pl.ds(t0, n)], rs_s.at[d, c], rs_r.at[d, c], side[d])

    def cols_of(a):
        return pl.ds(a * half_cols, half_cols)

    def keep(c):
        a, r0, nr = CHUNKS[c]
        return pltpu.make_async_copy(
            xnew.at[a, pl.ds(r0, nr)], out.at[0, pl.ds(r0, nr), cols_of(a)], out_sem.at[c])

    def keep_next(c):
        a, r0, nr = CHUNKS[c]
        return remote(
            xnew.at[a, pl.ds(r0, nr)], out.at[0, pl.ds(r0, nr), cols_of(a)],
            os_s.at[c], os_r.at[c], (p, w_next, h))

    def near(c):
        t0, n = span(c)
        cells = slice(t0, t0 + n)
        if not direct_sum(c):
            for copy in far_shares(c):
                copy.wait_recv()
        for d in (RIGHT, LEFT):
            if direct_sum(c):
                gsend[d, cells] = gside[d, cells].astype(BF16)
            else:
                mid = slice(d * half_cut, (d + 1) * half_cut)
                rest = slice((1 - d) * half_cut, (2 - d) * half_cut)
                gsend[d, cells, mid] = (gside[d, cells, mid] + r2[d, cells].astype(F32)).astype(BF16)
                gsend[d, cells, rest] = gside[d, cells, rest].astype(BF16)
            near_share(c, d).start()

    def finish(c):
        a, r0, nr = CHUNKS[c]
        t0, n = span(c)
        cells = slice(t0, t0 + n)
        total = xin[a, r0:r0 + nr, :, lanes(h)].reshape(n, cut).astype(F32) + gown[cells]
        for d in (RIGHT, LEFT):
            near_share(c, d).wait_recv()
            total = total + grecv[d, cells].astype(F32)
        if direct_sum(c):
            far_shares(c)[0].wait_recv()
            total = total + rfar[...].astype(F32)
        xnew[a, r0:r0 + nr] = total.astype(BF16).reshape(nr, half_cols, cut)

        @pl.when(p < n_pipe - 1)
        def _():
            hand_on(c).start()

        if a == 1:
            keep(c).start()
        else:
            @pl.when(odd == 0)
            def _():
                keep(c).start()

            @pl.when(odd == 1)
            def _():
                keep_next(c).start()

    def send_far(c):
        for copy in far_shares(c):
            copy.start()

    for a in range(2):
        cells = slice(a * half, (a + 1) * half)
        attend(a)
        g2[cells] = project(a, far).astype(BF16)
        if a == 0:
            for c in range(FIRST_OF_1):
                send_far(c)
        gside[RIGHT, cells] = project(a, right)
        gside[LEFT, cells] = project(a, left)
        if a == 0:
            near(0)
        gown[cells] = project(a, h)

    for i in range(1, COUNT + 2):
        if i < COUNT:
            near(i)
        ahead = i + FIRST_OF_1 - 1
        if ahead < COUNT:
            send_far(ahead)
        if i == 1:
            finish(0)
        if i >= 3:
            finish(i - 2)

    for c in range(COUNT):
        for d in (RIGHT, LEFT):
            near_share(c, d).wait_send()
        for copy in far_shares(c):
            copy.wait_send()

        @pl.when(p < n_pipe - 1)
        def _():
            hand_on(c).wait_send()

        if CHUNKS[c][0] == 1:
            keep(c).wait()
        else:
            @pl.when(odd == 0)
            def _():
                keep(c).wait()

            @pl.when(odd == 1)
            def _():
                keep_next(c).wait_send()
                keep_next(c).wait_recv()


def solution(mesh):
    sizes = tuple(mesh.shape[name] for name in ("pipe", "win", "head"))

    def per_device(stream, score_scale, value_weight, out_weight):
        my_rows, cols, width = stream.shape
        rows, half_cols, cut = my_rows * sizes[2], cols // 2, width // sizes[2]
        cells = rows * cols
        anywhere = pl.BlockSpec(memory_space=pl.ANY)
        dma = pltpu.SemaphoreType.DMA
        return pl.pallas_call(
            functools.partial(kernel, sizes),
            out_shape=jax.ShapeDtypeStruct((1, rows, cols, cut), BF16),
            in_specs=[anywhere, pl.BlockSpec(memory_space=pltpu.VMEM), anywhere, anywhere],
            out_specs=anywhere,
            scratch_shapes=[
                pltpu.VMEM((2, rows, half_cols, width), BF16),
                pltpu.VMEM((width, cut), BF16),
                pltpu.VMEM((cut, width), BF16),
                pltpu.VMEM((cells, cut), BF16),
                pltpu.VMEM((cells, cut), BF16),
                pltpu.VMEM((2, cells // 2, cut), BF16),
                pltpu.VMEM((cells, cut), BF16),
                pltpu.VMEM((2, cells, cut // 2), BF16),
                pltpu.VMEM((CHUNKS[0][2] * half_cols, cut), BF16),
                pltpu.VMEM((cells, cut), F32),
                pltpu.VMEM((2, cells, cut), F32),
                pltpu.VMEM((2, cells, cut), BF16),
                pltpu.VMEM((2, cells, cut), BF16),
                pltpu.VMEM((2, rows, half_cols, cut), BF16),
                dma((2,)), dma((2,)),
                dma((2, COUNT)), dma((2, COUNT)),
                dma((2, COUNT)), dma((2, COUNT)),
                dma((2, COUNT)), dma((2, COUNT)),
                dma((2, COUNT)), dma((2, COUNT)),
                dma((COUNT,)), dma((COUNT,)),
                dma((COUNT,)), dma((COUNT,)),
                dma((COUNT,)),
            ],
            compiler_params=pltpu.CompilerParams(collective_id=0, has_side_effects=True),
        )(stream, score_scale, value_weight, out_weight)

    return jax.shard_map(
        per_device,
        mesh=mesh,
        in_specs=(P("head", "win", None), P("pipe", None), P("pipe", None, "head"), P("pipe", "head", None)),
        out_specs=P("pipe", None, "win", "head"),
        check_vma=False,
    )
```

```python
import functools
import math

import jax
import jax.numpy as jnp
from jax import lax
from jax.experimental import pallas as pl
from jax.experimental.pallas import tpu as pltpu
from jax.sharding import PartitionSpec as P

MESH = pl.DeviceIdType.MESH
HEAD_DIM = 128
EPSILON = 1e-06
BF16, F32 = jnp.bfloat16, jnp.float32

CHUNKS = ((0, 0, 2), (0, 2, 2), (0, 4, 2), (0, 6, 2), (1, 0, 2), (1, 2, 2), (1, 4, 2), (1, 6, 2))
COUNT = len(CHUNKS)
FIRST_OF_1 = next(c for c in range(COUNT) if CHUNKS[c][0] == 1)
HALVES = (range(FIRST_OF_1), range(FIRST_OF_1, COUNT))
PEERS = (2, 1, 3)


def kernel(
    sizes, stream, scale, wv_hbm, wo_hbm, out,
    xin, wv, wo, ubuf, vbuf, obuf, gown, gsend, grecv, xnew,
    w_sem, own_sem, ag_s, ag_r, rs_s, rs_r, pp_s, pp_r, os_s, os_r, out_sem,
):
    n_pipe, n_win, n_head = sizes
    rows, half_cols, width = xin.shape[1:]
    cut = width // n_head
    heads = cut // HEAD_DIM
    half = rows * half_cols
    my_rows = stream.shape[0]
    p, w, h = lax.axis_index("pipe"), lax.axis_index("win"), lax.axis_index("head")
    odd = lax.rem(p, 2)
    peer = [lax.rem(h + k, n_head) for k in PEERS]
    w_next, w_prev = lax.rem(w + 1, n_win), lax.rem(w + n_win - 1, n_win)
    w_to = lax.rem(w + n_win - 1 + 2 * odd, n_win)
    w_from = lax.rem(w + n_win - 1 + 2 * odd, n_win)
    def lanes(k):
        return pl.ds(pl.multiple_of(k * cut, cut), cut)

    def remote(src, dst, s_sem, r_sem, to):
        return pltpu.make_async_remote_copy(
            src_ref=src, dst_ref=dst, send_sem=s_sem, recv_sem=r_sem, device_id=to, device_id_type=MESH)

    load_v = pltpu.make_async_copy(wv_hbm.at[0], wv, w_sem.at[0])
    load_o = pltpu.make_async_copy(wo_hbm.at[0], wo, w_sem.at[1])

    barrier = pltpu.get_barrier_semaphore()

    def greet(to):
        pl.semaphore_signal(barrier, inc=1, device_id=to, device_id_type=MESH)

    for k in peer:
        greet((p, w, k))

    @pl.when(p == 0)
    def _():
        greet((1, w, peer[0]))

    @pl.when(p > 0)
    def _():
        greet((p - 1, w, h))
        greet((p - 1, w_from, h))

    @pl.when(odd == 1)
    def _():
        greet((p, w_prev, h))

    load_v.start()
    load_o.start()

    for k in range(n_pipe):
        @pl.when(p == k)
        def _():
            pl.semaphore_wait(barrier, 3 + 2 * (k < n_pipe - 1) + k % 2 + (k == 1))

    def span(c):
        a, r0, nr = CHUNKS[c]
        return a * half + r0 * half_cols, nr * half_cols

    def normalize(a):
        x = xin[a].reshape(half, width).astype(F32)
        inverse = lax.rsqrt(jnp.sum(x * x, axis=1, keepdims=True) * (1.0 / width) + EPSILON)
        u = (x * inverse).astype(BF16)
        mine = xin[a, :, :, lanes(h)].reshape(half, cut).astype(F32)
        ubuf[a * half:(a + 1) * half, :] = (mine * inverse).astype(BF16)
        vbuf[a * half:(a + 1) * half, :] = jnp.dot(u, wv[...], preferred_element_type=F32).astype(BF16)

    def first_rows(a, d):
        cols = pl.ds(a * half_cols, half_cols)
        return remote(
            stream.at[:, cols], xin.at[a, pl.ds(h * my_rows, my_rows)],
            ag_s.at[d, a], ag_r.at[d, a], (0, w, peer[d]))

    @pl.when(p == 0)
    def _():
        own = [
            pltpu.make_async_copy(
                stream.at[:, pl.ds(a * half_cols, half_cols)], xin.at[a, pl.ds(h * my_rows, my_rows)], own_sem.at[a])
            for a in range(2)
        ]
        for a in range(2):
            for d in (1, 2):
                first_rows(a, d).start()
            own[a].start()
        load_v.wait()
        for a in range(2):
            own[a].wait()
            for d in range(3):
                first_rows(a, d).wait_recv()
            normalize(a)
        for a in range(2):
            for d in (1, 2):
                first_rows(a, d).wait_send()

    @pl.when(p == 1)
    def _():
        for a in range(2):
            first_rows(a, 0).start()
        for a in range(2):
            first_rows(a, 0).wait_send()

    def hand_on(c):
        a, r0, nr = CHUNKS[c]
        to = (p + 1, w_to if a == 0 else w, h)
        return remote(
            xnew.at[a, pl.ds(r0, nr)], xin.at[a, pl.ds(r0, nr), :, lanes(h)],
            pp_s.at[c], pp_r.at[c], to)

    @pl.when(p > 0)
    def _():
        def spread(c, d):
            a, r0, nr = CHUNKS[c]
            part = xin.at[a, pl.ds(r0, nr), :, lanes(h)]
            return remote(part, part, ag_s.at[d, c], ag_r.at[d, c], (p, w, peer[d]))

        load_v.wait()
        for c in range(COUNT):
            hand_on(c).wait_recv()
            for d in range(3):
                spread(c, d).start()
        for a in range(2):
            for c in HALVES[a]:
                for d in range(3):
                    spread(c, d).wait_recv()
            normalize(a)
        for c in range(COUNT):
            for d in range(3):
                spread(c, d).wait_send()

    load_o.wait()
    inv_root = 1.0 / math.sqrt(HEAD_DIM)

    def attend(a):
        for j in range(heads):
            col = slice(j * HEAD_DIM, (j + 1) * HEAD_DIM)
            gain = scale[:, pl.ds(pl.multiple_of(h * cut + j * HEAD_DIM, HEAD_DIM), HEAD_DIM)]
            q = (ubuf[a * half:(a + 1) * half, col].astype(F32) * gain).astype(BF16)
            s = lax.dot_general(q, ubuf[:, col], (((1,), (1,)), ((), ())), preferred_element_type=F32) * inv_root
            e = jnp.exp(s - jnp.max(s, axis=1, keepdims=True))
            prob = (e / jnp.sum(e, axis=1, keepdims=True)).astype(BF16)
            obuf[a, :, col] = jnp.dot(prob, vbuf[:, col], preferred_element_type=F32).astype(BF16)

    def project(a, k):
        return jnp.dot(obuf[a], wo[:, lanes(k)], preferred_element_type=F32)

    def share(c, d):
        t0, n = span(c)
        return remote(
            gsend.at[d, pl.ds(t0, n)], grecv.at[d, pl.ds(t0, n)], rs_s.at[d, c], rs_r.at[d, c], (p, w, peer[d]))

    def cols_of(a):
        return pl.ds(a * half_cols, half_cols)

    def keep(c):
        a, r0, nr = CHUNKS[c]
        return pltpu.make_async_copy(
            xnew.at[a, pl.ds(r0, nr)], out.at[0, pl.ds(r0, nr), cols_of(a)], out_sem.at[c])

    def keep_next(c):
        a, r0, nr = CHUNKS[c]
        return remote(
            xnew.at[a, pl.ds(r0, nr)], out.at[0, pl.ds(r0, nr), cols_of(a)],
            os_s.at[c], os_r.at[c], (p, w_next, h))

    def finish(c):
        a, r0, nr = CHUNKS[c]
        t0, n = span(c)
        cells = slice(t0, t0 + n)
        total = xin[a, r0:r0 + nr, :, lanes(h)].reshape(n, cut).astype(F32) + gown[cells]
        for d in range(3):
            share(c, d).wait_recv()
            total = total + grecv[d, cells].astype(F32)
        xnew[a, r0:r0 + nr] = total.astype(BF16).reshape(nr, half_cols, cut)

        @pl.when(p < n_pipe - 1)
        def _():
            hand_on(c).start()

        if a == 1:
            keep(c).start()
        else:
            @pl.when(odd == 0)
            def _():
                keep(c).start()

            @pl.when(odd == 1)
            def _():
                keep_next(c).start()

    for a in range(2):
        cells = slice(a * half, (a + 1) * half)
        attend(a)
        for d in range(3):
            gsend[d, cells] = project(a, peer[d]).astype(BF16)
        for c in HALVES[a]:
            for d in range(3):
                share(c, d).start()
        gown[cells] = project(a, h)

    for c in range(COUNT):
        finish(c)

    for c in range(COUNT):
        for d in range(3):
            share(c, d).wait_send()

        @pl.when(p < n_pipe - 1)
        def _():
            hand_on(c).wait_send()

        if CHUNKS[c][0] == 1:
            keep(c).wait()
        else:
            @pl.when(odd == 0)
            def _():
                keep(c).wait()

            @pl.when(odd == 1)
            def _():
                keep_next(c).wait_send()
                keep_next(c).wait_recv()


def solution(mesh):
    sizes = tuple(mesh.shape[name] for name in ("pipe", "win", "head"))

    def per_device(stream, score_scale, value_weight, out_weight):
        my_rows, cols, width = stream.shape
        rows, half_cols, cut = my_rows * sizes[2], cols // 2, width // sizes[2]
        cells = rows * cols
        anywhere = pl.BlockSpec(memory_space=pl.ANY)
        dma = pltpu.SemaphoreType.DMA
        return pl.pallas_call(
            functools.partial(kernel, sizes),
            out_shape=jax.ShapeDtypeStruct((1, rows, cols, cut), BF16),
            in_specs=[anywhere, pl.BlockSpec(memory_space=pltpu.VMEM), anywhere, anywhere],
            out_specs=anywhere,
            scratch_shapes=[
                pltpu.VMEM((2, rows, half_cols, width), BF16),
                pltpu.VMEM((width, cut), BF16),
                pltpu.VMEM((cut, width), BF16),
                pltpu.VMEM((cells, cut), BF16),
                pltpu.VMEM((cells, cut), BF16),
                pltpu.VMEM((2, cells // 2, cut), BF16),
                pltpu.VMEM((cells, cut), F32),
                pltpu.VMEM((3, cells, cut), BF16),
                pltpu.VMEM((3, cells, cut), BF16),
                pltpu.VMEM((2, rows, half_cols, cut), BF16),
                dma((2,)), dma((2,)),
                dma((3, COUNT)), dma((3, COUNT)),
                dma((3, COUNT)), dma((3, COUNT)),
                dma((COUNT,)), dma((COUNT,)),
                dma((COUNT,)), dma((COUNT,)),
                dma((COUNT,)),
            ],
            compiler_params=pltpu.CompilerParams(collective_id=0, has_side_effects=True),
        )(stream, score_scale, value_weight, out_weight)

    return jax.shard_map(
        per_device,
        mesh=mesh,
        in_specs=(P("head", "win", None), P("pipe", None), P("pipe", None, "head"), P("pipe", "head", None)),
        out_specs=P("pipe", None, "win", "head"),
        check_vma=False,
    )
```

```python
import functools
import math

import jax
import jax.numpy as jnp
from jax import lax
from jax.experimental import pallas as pl
from jax.experimental.pallas import tpu as pltpu
from jax.sharding import PartitionSpec as P

MESH = pl.DeviceIdType.MESH
HEAD_DIM = 128
EPSILON = 1e-06
BF16, F32 = jnp.bfloat16, jnp.float32

CHUNKS = tuple((a, r, 1) for a in range(2) for r in range(8))
COUNT = len(CHUNKS)
FIRST_OF_1 = next(c for c in range(COUNT) if CHUNKS[c][0] == 1)
HALVES = (range(FIRST_OF_1), range(FIRST_OF_1, COUNT))
PEERS = (2, 1, 3)


def kernel(
    sizes, stream, scale, wv_hbm, wo_hbm, out,
    xin, wv, wo, ubuf, vbuf, obuf, gown, gsend, grecv, xnew, via,
    w_sem, own_sem, ag_s, ag_r, v1_s, v1_r, v2_s, v2_r, rs_s, rs_r, pp_s, pp_r, os_s, os_r, out_sem,
):
    n_pipe, n_win, n_head = sizes
    rows, half_cols, width = xin.shape[1:]
    cut = width // n_head
    heads = cut // HEAD_DIM
    half = rows * half_cols
    my_rows = stream.shape[0]
    p, w, h = lax.axis_index("pipe"), lax.axis_index("win"), lax.axis_index("head")
    odd = lax.rem(p, 2)
    peer = [lax.rem(h + k, n_head) for k in PEERS]
    w_next, w_prev = lax.rem(w + 1, n_win), lax.rem(w + n_win - 1, n_win)
    w_to = lax.rem(w + n_win - 1 + 2 * odd, n_win)
    w_from = lax.rem(w + n_win - 1 + 2 * odd, n_win)
    def lanes(k):
        return pl.ds(pl.multiple_of(k * cut, cut), cut)

    def remote(src, dst, s_sem, r_sem, to):
        return pltpu.make_async_remote_copy(
            src_ref=src, dst_ref=dst, send_sem=s_sem, recv_sem=r_sem, device_id=to, device_id_type=MESH)

    load_v = pltpu.make_async_copy(wv_hbm.at[0], wv, w_sem.at[0])
    load_o = pltpu.make_async_copy(wo_hbm.at[0], wo, w_sem.at[1])

    barrier = pltpu.get_barrier_semaphore()

    def greet(to):
        pl.semaphore_signal(barrier, inc=1, device_id=to, device_id_type=MESH)

    for k in peer:
        greet((p, w, k))

    @pl.when(p == 0)
    def _():
        greet((1, w, h))
        greet((3, w, h))

    @pl.when(p > 0)
    def _():
        greet((p - 1, w, h))
        greet((p - 1, w_from, h))

    @pl.when(odd == 1)
    def _():
        greet((p, w_prev, h))

    load_v.start()
    load_o.start()

    for k in range(n_pipe):
        @pl.when(p == k)
        def _():
            pl.semaphore_wait(barrier, 3 + 2 * (k < n_pipe - 1) + 2 * (k % 2))

    def span(c):
        a, r0, nr = CHUNKS[c]
        return a * half + r0 * half_cols, nr * half_cols

    def normalize(a):
        x = xin[a].reshape(half, width).astype(F32)
        inverse = lax.rsqrt(jnp.sum(x * x, axis=1, keepdims=True) * (1.0 / width) + EPSILON)
        u = (x * inverse).astype(BF16)
        mine = xin[a, :, :, lanes(h)].reshape(half, cut).astype(F32)
        ubuf[a * half:(a + 1) * half, :] = (mine * inverse).astype(BF16)
        vbuf[a * half:(a + 1) * half, :] = jnp.dot(u, wv[...], preferred_element_type=F32).astype(BF16)

    def cols_of(a):
        return pl.ds(a * half_cols, half_cols)

    def first_rows(a, d):
        return remote(
            stream.at[:, cols_of(a)], xin.at[a, pl.ds(h * my_rows, my_rows)],
            ag_s.at[d, a], ag_r.at[d, a], (p, w, peer[d]))

    def cross(row):
        return remote(stream.at[pl.ds(row, 1), cols_of(1)], via, v1_s.at[0], v1_r.at[0], (p, w, peer[0]))

    def drop(row):
        return remote(via, xin.at[1, pl.ds(peer[0] * my_rows + row, 1)], v2_s.at[0], v2_r.at[row], (0, w, h))

    FIRST = ((0, (0, 1, 2)), (1, (1, 2)))

    @pl.when(p == 0)
    def _():
        own = [
            pltpu.make_async_copy(
                stream.at[:, cols_of(a)], xin.at[a, pl.ds(h * my_rows, my_rows)], own_sem.at[a])
            for a in range(2)
        ]
        for a, ways in FIRST:
            for d in ways:
                first_rows(a, d).start()
            own[a].start()
        load_v.wait()
        for a, ways in FIRST:
            own[a].wait()
            for d in ways:
                first_rows(a, d).wait_recv()
            if a == 1:
                for row in range(2):
                    drop(row).wait_recv()
            normalize(a)
        for a, ways in FIRST:
            for d in ways:
                first_rows(a, d).wait_send()

    for row in range(2):
        @pl.when(p == 2 * row + 1)
        def _():
            cross(row).start()
            cross(row).wait_recv()
            drop(row).start()
            cross(row).wait_send()
            drop(row).wait_send()

    def hand_on(c):
        a, r0, nr = CHUNKS[c]
        to = (p + 1, w_to if a == 0 else w, h)
        return remote(
            xnew.at[a, pl.ds(r0, nr)], xin.at[a, pl.ds(r0, nr), :, lanes(h)],
            pp_s.at[c], pp_r.at[c], to)

    @pl.when(p > 0)
    def _():
        def spread(c, d):
            a, r0, nr = CHUNKS[c]
            part = xin.at[a, pl.ds(r0, nr), :, lanes(h)]
            return remote(part, part, ag_s.at[d, c], ag_r.at[d, c], (p, w, peer[d]))

        load_v.wait()
        for c in range(COUNT):
            hand_on(c).wait_recv()
            for d in range(3):
                spread(c, d).start()
        for a in range(2):
            for c in HALVES[a]:
                for d in range(3):
                    spread(c, d).wait_recv()
            normalize(a)
        for c in range(COUNT):
            for d in range(3):
                spread(c, d).wait_send()

    load_o.wait()
    inv_root = 1.0 / math.sqrt(HEAD_DIM)

    def attend(a):
        for j in range(heads):
            col = slice(j * HEAD_DIM, (j + 1) * HEAD_DIM)
            gain = scale[:, pl.ds(pl.multiple_of(h * cut + j * HEAD_DIM, HEAD_DIM), HEAD_DIM)]
            q = (ubuf[a * half:(a + 1) * half, col].astype(F32) * gain).astype(BF16)
            s = lax.dot_general(q, ubuf[:, col], (((1,), (1,)), ((), ())), preferred_element_type=F32) * inv_root
            e = jnp.exp(s - jnp.max(s, axis=1, keepdims=True))
            prob = (e / jnp.sum(e, axis=1, keepdims=True)).astype(BF16)
            obuf[a, :, col] = jnp.dot(prob, vbuf[:, col], preferred_element_type=F32).astype(BF16)

    def project(a, k):
        return jnp.dot(obuf[a], wo[:, lanes(k)], preferred_element_type=F32)

    def share(c, d):
        t0, n = span(c)
        return remote(
            gsend.at[d, pl.ds(t0, n)], grecv.at[d, pl.ds(t0, n)], rs_s.at[d, c], rs_r.at[d, c], (p, w, peer[d]))

    def keep(c):
        a, r0, nr = CHUNKS[c]
        return pltpu.make_async_copy(
            xnew.at[a, pl.ds(r0, nr)], out.at[0, pl.ds(r0, nr), cols_of(a)], out_sem.at[c])

    def keep_next(c):
        a, r0, nr = CHUNKS[c]
        return remote(
            xnew.at[a, pl.ds(r0, nr)], out.at[0, pl.ds(r0, nr), cols_of(a)],
            os_s.at[c], os_r.at[c], (p, w_next, h))

    def finish(c):
        a, r0, nr = CHUNKS[c]
        t0, n = span(c)
        cells = slice(t0, t0 + n)
        total = xin[a, r0:r0 + nr, :, lanes(h)].reshape(n, cut).astype(F32) + gown[cells]
        for d in range(3):
            share(c, d).wait_recv()
            total = total + grecv[d, cells].astype(F32)
        xnew[a, r0:r0 + nr] = total.astype(BF16).reshape(nr, half_cols, cut)

        @pl.when(p < n_pipe - 1)
        def _():
            hand_on(c).start()

        if a == 1:
            keep(c).start()
        else:
            @pl.when(odd == 0)
            def _():
                keep(c).start()

            @pl.when(odd == 1)
            def _():
                keep_next(c).start()

    for a in range(2):
        cells = slice(a * half, (a + 1) * half)
        attend(a)
        for d in range(3):
            gsend[d, cells] = project(a, peer[d]).astype(BF16)
        for c in HALVES[a]:
            for d in range(3):
                share(c, d).start()
        gown[cells] = project(a, h)

    for c in range(COUNT):
        finish(c)

    for c in range(COUNT):
        for d in range(3):
            share(c, d).wait_send()

        @pl.when(p < n_pipe - 1)
        def _():
            hand_on(c).wait_send()

        if CHUNKS[c][0] == 1:
            keep(c).wait()
        else:
            @pl.when(odd == 0)
            def _():
                keep(c).wait()

            @pl.when(odd == 1)
            def _():
                keep_next(c).wait_send()
                keep_next(c).wait_recv()


def solution(mesh):
    sizes = tuple(mesh.shape[name] for name in ("pipe", "win", "head"))

    def per_device(stream, score_scale, value_weight, out_weight):
        my_rows, cols, width = stream.shape
        rows, half_cols, cut = my_rows * sizes[2], cols // 2, width // sizes[2]
        cells = rows * cols
        anywhere = pl.BlockSpec(memory_space=pl.ANY)
        dma = pltpu.SemaphoreType.DMA
        return pl.pallas_call(
            functools.partial(kernel, sizes),
            out_shape=jax.ShapeDtypeStruct((1, rows, cols, cut), BF16),
            in_specs=[anywhere, pl.BlockSpec(memory_space=pltpu.VMEM), anywhere, anywhere],
            out_specs=anywhere,
            scratch_shapes=[
                pltpu.VMEM((2, rows, half_cols, width), BF16),
                pltpu.VMEM((width, cut), BF16),
                pltpu.VMEM((cut, width), BF16),
                pltpu.VMEM((cells, cut), BF16),
                pltpu.VMEM((cells, cut), BF16),
                pltpu.VMEM((2, cells // 2, cut), BF16),
                pltpu.VMEM((cells, cut), F32),
                pltpu.VMEM((3, cells, cut), BF16),
                pltpu.VMEM((3, cells, cut), BF16),
                pltpu.VMEM((2, rows, half_cols, cut), BF16),
                pltpu.VMEM((1, half_cols, width), BF16),
                dma((2,)), dma((2,)),
                dma((3, COUNT)), dma((3, COUNT)),
                dma((1,)), dma((1,)), dma((1,)), dma((2,)),
                dma((3, COUNT)), dma((3, COUNT)),
                dma((COUNT,)), dma((COUNT,)),
                dma((COUNT,)), dma((COUNT,)),
                dma((COUNT,)),
            ],
            compiler_params=pltpu.CompilerParams(collective_id=0, has_side_effects=True),
        )(stream, score_scale, value_weight, out_weight)

    return jax.shard_map(
        per_device,
        mesh=mesh,
        in_specs=(P("head", "win", None), P("pipe", None), P("pipe", None, "head"), P("pipe", "head", None)),
        out_specs=P("pipe", None, "win", "head"),
        check_vma=False,
    )
```

```python
import functools
import math

import jax
import jax.numpy as jnp
from jax import lax
from jax.experimental import pallas as pl
from jax.experimental.pallas import tpu as pltpu
from jax.sharding import PartitionSpec as P

MESH = pl.DeviceIdType.MESH
HEAD_DIM = 128
EPSILON = 1e-06
BF16, F32 = jnp.bfloat16, jnp.float32

CHUNKS = tuple((a, r, 1) for a in range(2) for r in range(8))
COUNT = len(CHUNKS)
FIRST_OF_1 = next(c for c in range(COUNT) if CHUNKS[c][0] == 1)
HALVES = (range(FIRST_OF_1), range(FIRST_OF_1, COUNT))
PEERS = (2, 1, 3)
DETOUR = tuple(range(7))


def kernel(
    sizes, stream, scale, wv_hbm, wo_hbm, out,
    xin, wv, wo, ubuf, vbuf, obuf, gown, gsend, grecv, xnew, via, stop,
    w_sem, own_sem, ag_s, ag_r, v1_s, v1_r, v2_s, v2_r, m1_s, m1_r, m2_s, rs_s, rs_r, pp_s, pp_r, os_s, os_r, out_sem,
):
    n_pipe, n_win, n_head = sizes
    rows, half_cols, width = xin.shape[1:]
    cut = width // n_head
    heads = cut // HEAD_DIM
    half = rows * half_cols
    my_rows = stream.shape[0]
    p, w, h = lax.axis_index("pipe"), lax.axis_index("win"), lax.axis_index("head")
    odd = lax.rem(p, 2)
    peer = [lax.rem(h + k, n_head) for k in PEERS]
    w_next, w_prev = lax.rem(w + 1, n_win), lax.rem(w + n_win - 1, n_win)
    w_to = lax.rem(w + n_win + 1 - 2 * odd, n_win)
    w_from = lax.rem(w + n_win + 1 - 2 * odd, n_win)
    def lanes(k):
        return pl.ds(pl.multiple_of(k * cut, cut), cut)

    def remote(src, dst, s_sem, r_sem, to):
        return pltpu.make_async_remote_copy(
            src_ref=src, dst_ref=dst, send_sem=s_sem, recv_sem=r_sem, device_id=to, device_id_type=MESH)

    load_v = pltpu.make_async_copy(wv_hbm.at[0], wv, w_sem.at[0])
    load_o = pltpu.make_async_copy(wo_hbm.at[0], wo, w_sem.at[1])

    barrier = pltpu.get_barrier_semaphore()

    def greet(to):
        pl.semaphore_signal(barrier, inc=1, device_id=to, device_id_type=MESH)

    for k in peer:
        greet((p, w, k))

    @pl.when(p == n_pipe - 2)
    def _():
        greet((p + 1, w, peer[0]))

    @pl.when(p == 0)
    def _():
        greet((1, w, h))
        greet((3, w, h))

    @pl.when(p > 0)
    def _():
        greet((p - 1, w, h))
        greet((p - 1, w_from, h))

    @pl.when(odd == 1)
    def _():
        greet((p, w_next, h))

    load_v.start()
    load_o.start()

    for k in range(n_pipe):
        @pl.when(p == k)
        def _():
            pl.semaphore_wait(barrier, 3 + 2 * (k < n_pipe - 1) + 2 * (k % 2) + (k == n_pipe - 1))

    def span(c):
        a, r0, nr = CHUNKS[c]
        return a * half + r0 * half_cols, nr * half_cols

    def normalize(a):
        x = xin[a].reshape(half, width).astype(F32)
        inverse = lax.rsqrt(jnp.sum(x * x, axis=1, keepdims=True) * (1.0 / width) + EPSILON)
        u = (x * inverse).astype(BF16)
        mine = xin[a, :, :, lanes(h)].reshape(half, cut).astype(F32)
        ubuf[a * half:(a + 1) * half, :] = (mine * inverse).astype(BF16)
        vbuf[a * half:(a + 1) * half, :] = jnp.dot(u, wv[...], preferred_element_type=F32).astype(BF16)

    def cols_of(a):
        return pl.ds((1 - a) * half_cols, half_cols)

    def first_rows(a, d):
        return remote(
            stream.at[:, cols_of(a)], xin.at[a, pl.ds(h * my_rows, my_rows)],
            ag_s.at[d, a], ag_r.at[d, a], (p, w, peer[d]))

    def cross(row):
        return remote(stream.at[pl.ds(row, 1), cols_of(1)], via, v1_s.at[0], v1_r.at[0], (p, w, peer[0]))

    def drop(row):
        return remote(via, xin.at[1, pl.ds(peer[0] * my_rows + row, 1)], v2_s.at[0], v2_r.at[row], (0, w, h))

    FIRST = ((0, (0, 1, 2)), (1, (1, 2)))

    @pl.when(p == 0)
    def _():
        own = [
            pltpu.make_async_copy(
                stream.at[:, cols_of(a)], xin.at[a, pl.ds(h * my_rows, my_rows)], own_sem.at[a])
            for a in range(2)
        ]
        for a, ways in FIRST:
            for d in ways:
                first_rows(a, d).start()
            own[a].start()
        load_v.wait()
        for a, ways in FIRST:
            own[a].wait()
            for d in ways:
                first_rows(a, d).wait_recv()
            if a == 1:
                for row in range(2):
                    drop(row).wait_recv()
            normalize(a)
        for a, ways in FIRST:
            for d in ways:
                first_rows(a, d).wait_send()

    for row in range(2):
        @pl.when(p == 2 * row + 1)
        def _():
            cross(row).start()
            cross(row).wait_recv()
            drop(row).start()
            cross(row).wait_send()
            drop(row).wait_send()

    def hand_on(c):
        a, r0, nr = CHUNKS[c]
        to = (p + 1, w_to if a == 0 else w, h)
        return remote(
            xnew.at[a, pl.ds(r0, nr)], xin.at[a, pl.ds(r0, nr), :, lanes(h)],
            pp_s.at[c], pp_r.at[c], to)

    @pl.when(p > 0)
    def _():
        def spread(c, d):
            a, r0, nr = CHUNKS[c]
            part = xin.at[a, pl.ds(r0, nr), :, lanes(h)]
            return remote(part, part, ag_s.at[d, c], ag_r.at[d, c], (p, w, peer[d]))

        load_v.wait()
        for c in range(COUNT):
            hand_on(c).wait_recv()
            for d in range(3):
                spread(c, d).start()
        for a in range(2):
            for c in HALVES[a]:
                for d in range(3):
                    spread(c, d).wait_recv()
            normalize(a)
        for c in range(COUNT):
            for d in range(3):
                spread(c, d).wait_send()

    load_o.wait()
    inv_root = 1.0 / math.sqrt(HEAD_DIM)

    def attend(a):
        for j in range(heads):
            col = slice(j * HEAD_DIM, (j + 1) * HEAD_DIM)
            gain = scale[:, pl.ds(pl.multiple_of(h * cut + j * HEAD_DIM, HEAD_DIM), HEAD_DIM)]
            q = (ubuf[a * half:(a + 1) * half, col].astype(F32) * gain).astype(BF16)
            s = lax.dot_general(q, ubuf[:, col], (((1,), (1,)), ((), ())), preferred_element_type=F32) * inv_root
            e = jnp.exp(s - jnp.max(s, axis=1, keepdims=True))
            prob = (e / jnp.sum(e, axis=1, keepdims=True)).astype(BF16)
            obuf[a, :, col] = jnp.dot(prob, vbuf[:, col], preferred_element_type=F32).astype(BF16)

    def project(a, k):
        return jnp.dot(obuf[a], wo[:, lanes(k)], preferred_element_type=F32)

    def share(c, d):
        t0, n = span(c)
        return remote(
            gsend.at[d, pl.ds(t0, n)], grecv.at[d, pl.ds(t0, n)], rs_s.at[d, c], rs_r.at[d, c], (p, w, peer[d]))

    def detour(c):
        t0, n = span(c)
        return remote(
            gsend.at[0, pl.ds(t0, n)], stop.at[pl.ds(t0, n)], m1_s.at[c], m1_r.at[c], (n_pipe - 2, w, peer[0]))

    def rejoin(c):
        t0, n = span(c)
        return remote(
            stop.at[pl.ds(t0, n)], grecv.at[0, pl.ds(t0, n)], m2_s.at[c], rs_r.at[0, c], (n_pipe - 1, w, h))

    def keep(c):
        a, r0, nr = CHUNKS[c]
        return pltpu.make_async_copy(
            xnew.at[a, pl.ds(r0, nr)], out.at[0, pl.ds(r0, nr), cols_of(a)], out_sem.at[c])

    def keep_next(c):
        a, r0, nr = CHUNKS[c]
        return remote(
            xnew.at[a, pl.ds(r0, nr)], out.at[0, pl.ds(r0, nr), cols_of(a)],
            os_s.at[c], os_r.at[c], (p, w_prev, h))

    def finish(c):
        a, r0, nr = CHUNKS[c]
        t0, n = span(c)
        cells = slice(t0, t0 + n)
        total = xin[a, r0:r0 + nr, :, lanes(h)].reshape(n, cut).astype(F32) + gown[cells]
        for d in range(3):
            share(c, d).wait_recv()
            total = total + grecv[d, cells].astype(F32)
        xnew[a, r0:r0 + nr] = total.astype(BF16).reshape(nr, half_cols, cut)

        @pl.when(p < n_pipe - 1)
        def _():
            hand_on(c).start()

        if a == 1:
            keep(c).start()
        else:
            @pl.when(odd == 0)
            def _():
                keep(c).start()

            @pl.when(odd == 1)
            def _():
                keep_next(c).start()

    for a in range(2):
        cells = slice(a * half, (a + 1) * half)
        attend(a)
        for d in range(3):
            gsend[d, cells] = project(a, peer[d]).astype(BF16)
        for c in HALVES[a]:
            if c in DETOUR:
                @pl.when(p < n_pipe - 1)
                def _():
                    share(c, 0).start()

                @pl.when(p == n_pipe - 1)
                def _():
                    detour(c).start()
            for d in range(1 if c in DETOUR else 0, 3):
                share(c, d).start()
        gown[cells] = project(a, h)

    for c in range(COUNT):
        finish(c)

    for c in range(COUNT):
        if c in DETOUR:
            @pl.when(p < n_pipe - 1)
            def _():
                share(c, 0).wait_send()

            @pl.when(p == n_pipe - 1)
            def _():
                detour(c).wait_send()
        for d in range(1 if c in DETOUR else 0, 3):
            share(c, d).wait_send()

        @pl.when(p < n_pipe - 1)
        def _():
            hand_on(c).wait_send()

        if CHUNKS[c][0] == 1:
            keep(c).wait()
        else:
            @pl.when(odd == 0)
            def _():
                keep(c).wait()

            @pl.when(odd == 1)
            def _():
                keep_next(c).wait_send()
                keep_next(c).wait_recv()

    @pl.when(p == n_pipe - 2)
    def _():
        for c in DETOUR:
            detour(c).wait_recv()
            rejoin(c).start()
        for c in DETOUR:
            rejoin(c).wait_send()


def solution(mesh):
    sizes = tuple(mesh.shape[name] for name in ("pipe", "win", "head"))

    def per_device(stream, score_scale, value_weight, out_weight):
        my_rows, cols, width = stream.shape
        rows, half_cols, cut = my_rows * sizes[2], cols // 2, width // sizes[2]
        cells = rows * cols
        anywhere = pl.BlockSpec(memory_space=pl.ANY)
        dma = pltpu.SemaphoreType.DMA
        return pl.pallas_call(
            functools.partial(kernel, sizes),
            out_shape=jax.ShapeDtypeStruct((1, rows, cols, cut), BF16),
            in_specs=[anywhere, pl.BlockSpec(memory_space=pltpu.VMEM), anywhere, anywhere],
            out_specs=anywhere,
            scratch_shapes=[
                pltpu.VMEM((2, rows, half_cols, width), BF16),
                pltpu.VMEM((width, cut), BF16),
                pltpu.VMEM((cut, width), BF16),
                pltpu.VMEM((cells, cut), BF16),
                pltpu.VMEM((cells, cut), BF16),
                pltpu.VMEM((2, cells // 2, cut), BF16),
                pltpu.VMEM((cells, cut), F32),
                pltpu.VMEM((3, cells, cut), BF16),
                pltpu.VMEM((3, cells, cut), BF16),
                pltpu.VMEM((2, rows, half_cols, cut), BF16),
                pltpu.VMEM((1, half_cols, width), BF16),
                pltpu.VMEM((cells, cut), BF16),
                dma((2,)), dma((2,)),
                dma((3, COUNT)), dma((3, COUNT)),
                dma((1,)), dma((1,)), dma((1,)), dma((2,)),
                dma((COUNT,)), dma((COUNT,)), dma((COUNT,)),
                dma((3, COUNT)), dma((3, COUNT)),
                dma((COUNT,)), dma((COUNT,)),
                dma((COUNT,)), dma((COUNT,)),
                dma((COUNT,)),
            ],
            compiler_params=pltpu.CompilerParams(collective_id=0, has_side_effects=True),
        )(stream, score_scale, value_weight, out_weight)

    return jax.shard_map(
        per_device,
        mesh=mesh,
        in_specs=(P("head", "win", None), P("pipe", None), P("pipe", None, "head"), P("pipe", "head", None)),
        out_specs=P("pipe", None, "win", "head"),
        check_vma=False,
    )
```
